32 devices in a mesh: grp: 1, row: 32 (over z, y, x, core), col: 1.
Axes of the slice: x: 2, y: 2, z: 4, core: 2. Of those that a mesh axis runs over, the one named last changes fastest.
Arguments:
- pair_map: bfloat16 [128, 128, 288], P(('grp', 'row'), 'col'), may hold values from -6 to 6
- norm_in: float32 [288], replicated, may hold values from 0.1 to 1.9
- w_query: bfloat16 [288, 256], replicated, may hold values from -12 to 12
- w_key: bfloat16 [288, 256], replicated, may hold values from -1 to 1
- w_value: bfloat16 [288, 256], replicated, may hold values from -0.375 to 0.375
- w_gate: bfloat16 [288, 256], replicated, may hold values from -0.375 to 0.375
- w_out: bfloat16 [256, 288], replicated, may hold values from -3 to 3
- norm_mid: float32 [288], replicated, may hold values from 0.1 to 1.9
- norm_out: float32 [288], replicated, may hold values from 0.1 to 1.9
- w_up: bfloat16 [288, 1152], replicated, may hold values from -0.375 to 0.375
- w_down: bfloat16 [1152, 288], replicated, may hold values from -0.1875 to 0.1875
Outputs:
- updated: bfloat16 [128, 128, 288], P(('grp', 'row'), 'col')
The draws below stay inside these ranges and needn't reach their ends.
All inputs are finite; a program needn't handle non-finite values.
Results may differ from the reference program's by a relative error of at most 0.014.
Values may be sent and summed in bfloat16 or wider, within the bound.
A program may use at most 64 MiB of HBM per device.

```python
import jax
import jax.numpy as jnp
from jax import lax

C = 288
HEADS = 8
HEAD_DIM = 32
FF = 1152
HD = 256
L = 128


def shared_base(key):
    return jax.random.truncated_normal(jax.random.fold_in(key, 7), -6.0, 6.0, (C, HD), jnp.float32) * C ** (-0.5)


def draw_w_key(key, part):
    return shared_base(key).astype(jnp.bfloat16)


def draw_w_query(key, part):
    independent = jax.random.truncated_normal(jax.random.fold_in(key, 11), -6.0, 6.0, (C, HD), jnp.float32) * C ** (-0.5)
    exponent = jax.random.uniform(jax.random.fold_in(key, 17), (HEADS,), jnp.float32, 0.0, jnp.log(2.5))
    temper = jnp.repeat(jnp.exp(exponent), HEAD_DIM)
    return (independent * temper[None, :]).astype(jnp.bfloat16)


def block_scale(own_key, extent, split, low, top_value):
    level, own = 1.0, jax.random.fold_in(own_key, 6)
    for position, shards_of in split:
        heights = jnp.exp(jax.random.uniform(jax.random.fold_in(own, position), (shards_of,), jnp.float32, low / len(split), top_value / len(split)))
        level = level * jnp.repeat(heights, extent[position] // shards_of).reshape([-1 if axis == position else 1 for axis in range(len(extent))])
    return level


def scatter_about(rng, extent, spread, limit, cuts=(), dtype=jnp.bfloat16):
    values = jax.random.normal(rng, extent, jnp.float32) * spread
    if len(cuts) > 0:
        values = block_scale(rng, extent, cuts, -0.22, 0.18) * values
    return jnp.clip(values, min=-limit, max=limit).astype(dtype)


def setup_inputs(seed: int = 0, part: int = 0) -> dict:
    seeds = jax.random.split(jax.random.key(seed), 12)
    part_splits = jax.random.split(jax.random.fold_in(seeds[11], part), 12)
    return {
        "pair_map": scatter_about(part_splits[0], (L, L, C), 1.0, 6.0, ((0, 32),)),
        "norm_in": jnp.clip(1.0 + 0.18 * jax.random.normal(seeds[1], (C,), jnp.float32), 0.1, 1.9),
        "w_query": draw_w_query(jax.random.fold_in(seeds[11], 71), part),
        "w_key": draw_w_key(jax.random.fold_in(seeds[11], 71), part),
        "w_value": scatter_about(seeds[4], (C, HD), C ** -0.5, 0.375),
        "w_gate": scatter_about(seeds[5], (C, HD), C ** -0.5, 0.375),
        "w_out": scatter_about(seeds[6], (HD, C), (max(HD // 64, 1)) ** -0.5, 3.0),
        "norm_mid": jnp.clip(1.0 + 0.18 * jax.random.normal(seeds[7], (C,), jnp.float32), 0.1, 1.9),
        "norm_out": jnp.clip(1.0 + 0.18 * jax.random.normal(seeds[8], (C,), jnp.float32), 0.1, 1.9),
        "w_up": scatter_about(seeds[9], (C, FF), C ** -0.5, 0.375),
        "w_down": scatter_about(seeds[10], (FF, C), FF ** -0.5, 0.1875),
    }


epsilon = 1e-06

def normalize(inputs, gain):
    mean_square = lax.optimization_barrier(jnp.mean(inputs * inputs, axis=-1, keepdims=True))
    return inputs * lax.rsqrt(mean_square + epsilon) * gain

def attend_rows(pair_rows, norm_in, w_query, w_key, w_value, w_gate, w_out, norm_mid):
    row_count = pair_rows.shape[0]
    length = pair_rows.shape[1]
    channels = pair_rows.shape[2]
    widened = pair_rows.astype(jnp.float32)
    normed = normalize(widened, norm_in).astype(jnp.bfloat16).reshape(row_count * length, channels)

    def project(weight):
        return jnp.dot(normed, weight, preferred_element_type=jnp.float32).astype(jnp.bfloat16)
    query_rows = project(w_query).reshape(row_count, length, HEADS, HEAD_DIM).transpose(2, 0, 1, 3)
    key_rows = project(w_key).reshape(row_count, length, HEADS, HEAD_DIM).transpose(2, 0, 1, 3)
    value_rows = project(w_value).reshape(row_count, length, HEADS, HEAD_DIM).transpose(2, 0, 1, 3)
    gate_rows = project(w_gate)
    score_scale = HEAD_DIM ** (-0.5)

    def one_head(triple):
        query_head, key_head, value_head = triple
        scores = jnp.einsum('mqd,mkd->mqk', query_head.astype(jnp.float32), key_head.astype(jnp.float32)) * score_scale
        scores = scores - lax.optimization_barrier(jnp.max(scores, axis=-1, keepdims=True))
        expanded = jnp.exp(scores)
        probabilities = (expanded / lax.optimization_barrier(jnp.sum(expanded, axis=-1, keepdims=True))).astype(jnp.bfloat16)
        return jnp.einsum('mqk,mkd->mqd', probabilities.astype(jnp.float32), value_head.astype(jnp.float32))
    head_outputs = lax.map(one_head, (query_rows, key_rows, value_rows))
    merged = head_outputs.transpose(1, 2, 0, 3).reshape(row_count * length, HEADS * HEAD_DIM)
    gated = (merged * jax.nn.sigmoid(gate_rows.astype(jnp.float32))).astype(jnp.bfloat16)
    update = jnp.dot(gated, w_out, preferred_element_type=jnp.float32).reshape(row_count, length, channels)
    return normalize(widened + update, norm_mid).astype(jnp.bfloat16)

def feed_forward(sym_rows, norm_out, w_up, w_down):
    shape_in = sym_rows.shape
    flat = sym_rows.reshape(-1, shape_in[-1]).astype(jnp.float32)
    normed = normalize(flat, norm_out).astype(jnp.bfloat16)
    hidden = jnp.maximum(jnp.dot(normed, w_up, preferred_element_type=jnp.float32), 0.0).astype(jnp.bfloat16)
    result = flat + jnp.dot(hidden, w_down, preferred_element_type=jnp.float32)
    return result.astype(jnp.bfloat16).reshape(shape_in)

def reference(pair_map, norm_in, w_query, w_key, w_value, w_gate, w_out, norm_mid, norm_out, w_up, w_down):
    length = pair_map.shape[0]
    channels = pair_map.shape[2]
    blocks = pair_map.reshape(length // 8, 8, length, channels)
    attended = lax.map(lambda block_rows: attend_rows(block_rows, norm_in, w_query, w_key, w_value, w_gate, w_out, norm_mid), blocks)
    attended = attended.reshape(length, length, channels)
    mirrored = jnp.transpose(attended, (1, 0, 2))
    symmetric = ((attended.astype(jnp.float32) + mirrored.astype(jnp.float32)) * 0.5).astype(jnp.bfloat16)
    output = lax.map(lambda block_rows: feed_forward(block_rows, norm_out, w_up, w_down), symmetric.reshape(length // 8, 8, length, channels))
    return output.reshape(length, length, channels)
```

```python
import functools

import jax
import jax.numpy as jnp
from jax import lax
from jax.experimental import pallas as pl
from jax.experimental.pallas import tpu as pltpu
from jax.sharding import PartitionSpec as P

HEADS = 8
HEAD_DIM = 32
LANES = 128
LOG2E = 1.4426950408889634
MIB = 1 << 20

epsilon = 1e-06


def normalize(inputs, gain):
    mean_square = jnp.mean(inputs * inputs, axis=0, keepdims=True)
    return inputs * lax.rsqrt(mean_square + epsilon) * gain


def contract(left, right, left_dim, right_dim):
    return lax.dot_general(
        left, right, (((left_dim,), (right_dim,)), ((), ())), preferred_element_type=jnp.float32
    )


def upright(gain, pairs):
    column = jnp.broadcast_to(gain[None], (LANES, gain.shape[0])).T
    return jnp.concatenate([column] * (pairs // LANES), axis=1)


def identity(size):
    row = lax.broadcasted_iota(jnp.int32, (size, size), 0)
    column = lax.broadcasted_iota(jnp.int32, (size, size), 1)
    return jnp.where(row == column, 1.0, 0.0).astype(jnp.bfloat16)


def mirrored(own_rows, length):
    shape = (own_rows * length, own_rows * length)
    slot = lax.broadcasted_iota(jnp.int32, shape, 0)
    pair = lax.broadcasted_iota(jnp.int32, shape, 1)
    column = pair % length
    wanted = column % own_rows * length + column // own_rows * own_rows + pair // length
    return jnp.where(slot == wanted, 1.0, 0.0).astype(jnp.bfloat16)


def block_kernel(
    count,
    cols,
    x_hbm,
    norm_in_hbm,
    w_query_hbm,
    w_key_hbm,
    w_value_hbm,
    w_gate_hbm,
    w_out_hbm,
    norm_mid_hbm,
    norm_out_hbm,
    w_up_hbm,
    w_down_hbm,
    out_ref,
    x_ref,
    norm_in,
    w_query,
    w_key,
    w_value,
    w_gate,
    w_out,
    norm_mid,
    norm_out,
    w_up,
    w_down,
    turned_ref,
    query_ref,
    key_ref,
    value_ref,
    gate_ref,
    merged_ref,
    own_ref,
    gain_ref,
    rest_ref,
    mirror_ref,
    up_ref,
    send_ref,
    land_ref,
    load_sem,
    send_sem,
    recv_sem,
):
    own_rows, channels, length = x_ref.shape
    phase_rows = query_ref.shape[0]
    phase_pairs = phase_rows * length
    groups = send_ref.shape[1]
    full = channels // LANES
    rest = channels - full * LANES
    extra = groups - own_rows * full
    halves = recv_sem.shape[0]
    part_count = count // halves
    part = length // halves
    me = lax.axis_index("row") * cols + lax.axis_index("col")
    my_half = me // part_count

    def place(other):
        return {"row": other // cols, "col": lax.rem(other, cols)}

    def another(step):
        return jnp.where(step < me, step, step + 1)

    def transfer(row, size, source, target, other, half):
        span = pl.ds(row * full, size)
        return pltpu.make_async_remote_copy(
            src_ref=send_ref.at[source, span],
            dst_ref=land_ref.at[target, span],
            send_sem=send_sem,
            recv_sem=recv_sem.at[half],
            device_id=place(other),
            device_id_type=pl.DeviceIdType.MESH,
        )

    loads = [
        pltpu.make_async_copy(source, target, load_sem.at[index])
        for index, (source, target) in enumerate(
            [
                (x_hbm, x_ref),
                (norm_in_hbm, norm_in),
                (w_query_hbm, w_query),
                (w_value_hbm, w_value),
                (w_gate_hbm, w_gate),
                (w_key_hbm, w_key),
                (w_out_hbm, w_out),
                (norm_mid_hbm, norm_mid),
                (norm_out_hbm, norm_out),
                (w_up_hbm, w_up),
                (w_down_hbm, w_down),
            ]
        )
    ]
    for load in loads[:8]:
        load.start()
    barrier = pltpu.get_barrier_semaphore()

    @pl.loop(0, count - 1)
    def _(step):
        pl.semaphore_signal(
            barrier, inc=1, device_id=place(another(step)), device_id_type=pl.DeviceIdType.MESH
        )

    for load in loads[8:]:
        load.start()
    flip = identity(length)
    for load in loads[:8]:
        load.wait()
    gain_ref[0] = upright(norm_in[...], phase_pairs)
    gain_ref[1] = upright(norm_mid[...], phase_pairs)
    for index, weight in enumerate((w_query, w_value, w_gate)):
        turned_ref[index] = weight[...].T
    scale = HEAD_DIM ** (-0.5) * LOG2E
    fold = 2
    reach = LANES // HEAD_DIM
    nothing = jnp.zeros((HEAD_DIM, length), jnp.bfloat16)

    @pl.loop(0, own_rows)
    def _(row):
        @pl.when(lax.rem(row, phase_rows) == 0)
        def _():
            widened = jnp.concatenate(
                [x_ref[row + inside] for inside in range(phase_rows)], axis=1
            ).astype(jnp.float32)
            normed = normalize(widened, gain_ref[0]).astype(jnp.bfloat16)
            queries = contract(turned_ref[0], normed, 1, 0).astype(jnp.bfloat16)
            values = contract(turned_ref[1], normed, 1, 0).astype(jnp.bfloat16)
            gates = jax.nn.sigmoid(contract(turned_ref[2], normed, 1, 0))
            keys = contract(normed, w_key[...], 0, 0).astype(jnp.bfloat16)
            for inside in range(phase_rows):
                span = slice(inside * length, (inside + 1) * length)
                query_ref[inside] = queries[:, span]
                value_ref[inside] = values[:, span]
                gate_ref[inside] = gates[:, span]
                key_ref[inside] = keys[span]

        inside = lax.rem(row, phase_rows)
        for head in range(0, HEADS, fold):
            base = head // reach * reach
            spread = jnp.concatenate(
                [
                    jnp.concatenate(
                        [
                            query_ref[inside, other * HEAD_DIM : (other + 1) * HEAD_DIM]
                            if other == chosen
                            else nothing
                            for other in range(base, base + reach)
                        ],
                        axis=0,
                    )
                    for chosen in range(head, head + fold)
                ],
                axis=1,
            )
            group = slice(base * HEAD_DIM, (base + reach) * HEAD_DIM)
            scores = contract(key_ref[inside, :, group], spread, 1, 0)
            expanded = jnp.exp2((scores - jnp.max(scores, axis=0, keepdims=True)) * scale)
            inverse = 1.0 / jnp.sum(expanded, axis=0, keepdims=True)
            rounded = expanded.astype(jnp.bfloat16)
            for chosen in range(fold):
                span = slice((head + chosen) * HEAD_DIM, (head + chosen + 1) * HEAD_DIM)
                over = slice(chosen * length, (chosen + 1) * length)
                attended = contract(value_ref[inside, span], rounded[:, over], 1, 0)
                merged_ref[span] = (
                    attended * inverse[:, over] * gate_ref[inside, span]
                ).astype(jnp.bfloat16)
        update = contract(w_out[...], merged_ref[...], 1, 0)
        widened = x_ref[row].astype(jnp.float32)
        rowwise = normalize(widened + update, gain_ref[1, :, :length]).astype(jnp.bfloat16)
        own_ref[row] = rowwise
        if rest:
            rest_ref[row] = rowwise[full * LANES :]
        sent = contract(flip, rowwise[: full * LANES], 1, 1)
        for group in range(full):
            piece = sent[:, group * LANES : (group + 1) * LANES]
            send_ref[:, row * full + group] = piece.reshape(count, own_rows, LANES).astype(
                jnp.bfloat16
            )

        @pl.when(row == 0)
        def _():
            pl.semaphore_wait(barrier, count - 1)

        def send_all(size):
            @pl.loop(0, count - 1)
            def _(step):
                other = another(step)
                transfer(row, size, other, me, other, my_half).start()

        @pl.when(row < own_rows - 1)
        def _():
            send_all(full)

        @pl.when(row == own_rows - 1)
        def _():
            if rest:
                folded = rest_ref[...].reshape(own_rows * rest, length)
                for index in range(extra):
                    held = folded[index * LANES : (index + 1) * LANES]
                    send_ref[:, own_rows * full + index, :, : held.shape[0]] = (
                        contract(flip, held, 1, 1)
                        .reshape(count, own_rows, held.shape[0])
                        .astype(jnp.bfloat16)
                    )
            send_all(full + extra)

    keep = pltpu.make_async_copy(send_ref.at[me], land_ref.at[me], recv_sem.at[my_half])
    keep.start()
    mirror_ref[...] = mirrored(own_rows, part)
    for load in loads[8:]:
        load.wait()

    @pl.loop(0, w_up.shape[1] // LANES)
    def _(block):
        span = pl.ds(pl.multiple_of(block * LANES, LANES), LANES)
        up_ref[span, :] = w_up[:, span].T

    gain_out = upright(norm_out[...], LANES)[:, :1]
    whole = transfer(0, groups, pl.ds(0, count - 1), pl.ds(0, count - 1), another(0), 0)
    whole.wait_send()
    turn = identity(part)
    for half in range(halves):
        source = pl.ds(half * part_count, part_count)
        transfer(0, groups, source, source, another(0), half).wait_recv()

        def landed(group, half=half):
            block = land_ref[half * part_count : (half + 1) * part_count, group]
            return block.astype(jnp.float32).reshape(part, LANES)

        slots = jnp.concatenate(
            [
                jnp.concatenate([landed(row * full + group) for group in range(full)], axis=1)
                for row in range(own_rows)
            ],
            axis=0,
        ).astype(jnp.bfloat16)
        received = contract(slots, mirror_ref[...], 0, 0)
        if rest:
            per = LANES // rest
            pieces = []
            for index in range(extra):
                held = landed(own_rows * full + index).astype(jnp.bfloat16)
                upended = contract(held, turn, 0, 0).astype(jnp.bfloat16)
                for inside in range(min(per, own_rows - index * per)):
                    pieces.append(upended[inside * rest : (inside + 1) * rest])
            tail = contract(jnp.concatenate(pieces, axis=1), mirror_ref[...], 1, 0)
            received = jnp.concatenate([received, tail], axis=0)
        mine = jnp.concatenate(
            [own_ref[row, :, half * part : (half + 1) * part] for row in range(own_rows)], axis=1
        )
        symmetric = ((mine.astype(jnp.float32) + received) * 0.5).astype(jnp.bfloat16)
        flat = symmetric.astype(jnp.float32)
        inner = normalize(flat, gain_out).astype(jnp.bfloat16)
        hidden = jnp.maximum(contract(up_ref[...], inner, 1, 0), 0.0).astype(jnp.bfloat16)
        result = (flat + contract(w_down[...], hidden, 1, 0)).astype(jnp.bfloat16)
        for row in range(own_rows):
            out_ref[row, :, half * part : (half + 1) * part] = result[
                :, row * part : (row + 1) * part
            ]


def local(
    pair_map, norm_in, w_query, w_key, w_value, w_gate, w_out, norm_mid, norm_out, w_up, w_down
):
    cols = lax.axis_size("col")
    count = lax.axis_size("row") * cols
    tile_rows, tile_cols, channels = pair_map.shape
    own_rows = tile_rows // cols
    length = tile_cols * cols
    rows = pair_map
    if cols > 1:
        folds = pair_map.reshape(cols, own_rows, tile_cols, channels)
        rows = lax.all_to_all(folds, "col", split_axis=0, concat_axis=2, tiled=True)[0]
    width = w_query.shape[1]
    phase_rows = 2 if own_rows % 2 == 0 else 1
    halves = 2 if count % 2 == 0 else 1
    part_pairs = own_rows * length // halves
    rest = channels % LANES
    groups = own_rows * (channels // LANES)
    if rest:
        groups += pl.cdiv(own_rows, LANES // rest)
    operands = (
        rows.transpose(0, 2, 1),
        norm_in,
        w_query,
        w_key,
        w_value,
        w_gate,
        w_out.T,
        norm_mid,
        norm_out,
        w_up,
        w_down.T,
    )
    finished = pl.pallas_call(
        functools.partial(block_kernel, count, cols),
        out_shape=OUT((own_rows, channels, length), jnp.bfloat16),
        in_specs=[pl.BlockSpec(memory_space=pl.ANY)] * len(operands),
        out_specs=pl.BlockSpec(memory_space=pltpu.VMEM),
        scratch_shapes=[pltpu.VMEM(operand.shape, operand.dtype) for operand in operands]
        + [
            pltpu.VMEM((3, width, channels), jnp.bfloat16),
            pltpu.VMEM((phase_rows, width, length), jnp.bfloat16),
            pltpu.VMEM((phase_rows, length, width), jnp.bfloat16),
            pltpu.VMEM((phase_rows, width, length), jnp.bfloat16),
            pltpu.VMEM((phase_rows, width, length), jnp.float32),
            pltpu.VMEM((width, length), jnp.bfloat16),
            pltpu.VMEM((own_rows, channels, length), jnp.bfloat16),
            pltpu.VMEM((2, channels, phase_rows * length), jnp.float32),
            pltpu.VMEM((own_rows, max(rest, 16), length), jnp.bfloat16),
            pltpu.VMEM((part_pairs, part_pairs), jnp.bfloat16),
            pltpu.VMEM(w_up.shape[::-1], jnp.bfloat16),
            pltpu.VMEM((count, groups, own_rows, LANES), jnp.bfloat16),
            pltpu.VMEM((count, groups, own_rows, LANES), jnp.bfloat16),
            pltpu.SemaphoreType.DMA((len(operands),)),
            pltpu.SemaphoreType.DMA,
            pltpu.SemaphoreType.DMA((halves,)),
        ],
        compiler_params=pltpu.CompilerParams(
            collective_id=0, has_side_effects=True, vmem_limit_bytes=VLIM
        ),
    )(*operands).transpose(0, 2, 1)
    if cols == 1:
        return finished
    returned = lax.all_to_all(
        finished.reshape(own_rows, cols, tile_cols, channels),
        "col",
        split_axis=1,
        concat_axis=0,
        tiled=True,
    )
    return returned.reshape(tile_rows, tile_cols, channels)


VLIM = 62 * MIB
OUT = pltpu.VMEM


def solution(mesh):
    placed = (P(("grp", "row"), "col", None), P(), P(), P(), P(), P(), P(), P(), P(), P(), P())
    return jax.shard_map(
        local, mesh=mesh, in_specs=placed, out_specs=P(("grp", "row"), "col", None), check_vma=False
    )
```

```python
import functools

import jax
import jax.numpy as jnp
from jax import lax
from jax.experimental import pallas as pl
from jax.experimental.pallas import tpu as pltpu
from jax.sharding import PartitionSpec as P

HEADS = 8
HEAD_DIM = 32
LANES = 128
LOG2E = 1.4426950408889634
MIB = 1 << 20

epsilon = 1e-06


def normalize(inputs, gain):
    mean_square = jnp.mean(inputs * inputs, axis=0, keepdims=True)
    return inputs * lax.rsqrt(mean_square + epsilon) * gain


def contract(left, right, left_dim, right_dim):
    return lax.dot_general(
        left, right, (((left_dim,), (right_dim,)), ((), ())), preferred_element_type=jnp.float32
    )


def upright(gain, pairs):
    column = jnp.broadcast_to(gain[None], (LANES, gain.shape[0])).T
    return jnp.concatenate([column] * (pairs // LANES), axis=1)


def identity(size):
    row = lax.broadcasted_iota(jnp.int32, (size, size), 0)
    column = lax.broadcasted_iota(jnp.int32, (size, size), 1)
    return jnp.where(row == column, 1.0, 0.0).astype(jnp.bfloat16)


def mirrored(own_rows, length):
    shape = (own_rows * length, own_rows * length)
    slot = lax.broadcasted_iota(jnp.int32, shape, 0)
    pair = lax.broadcasted_iota(jnp.int32, shape, 1)
    column = pair % length
    wanted = column % own_rows * length + column // own_rows * own_rows + pair // length
    return jnp.where(slot == wanted, 1.0, 0.0).astype(jnp.bfloat16)


def block_kernel(
    count,
    cols,
    x_hbm,
    norm_in_hbm,
    w_query_hbm,
    w_key_hbm,
    w_value_hbm,
    w_gate_hbm,
    w_out_hbm,
    norm_mid_hbm,
    norm_out_hbm,
    w_up_hbm,
    w_down_hbm,
    out_ref,
    x_ref,
    norm_in,
    w_query,
    w_key,
    w_value,
    w_gate,
    w_out,
    norm_mid,
    norm_out,
    w_up,
    w_down,
    turned_ref,
    merged_ref,
    row_ref,
    own_ref,
    gain_ref,
    rest_ref,
    mirror_ref,
    up_ref,
    send_ref,
    land_ref,
    load_sem,
    send_sem,
    recv_sem,
    go_sem,
):
    own_rows, channels, length = x_ref.shape
    phase_rows = 2 if own_rows % 2 == 0 else 1
    phase_pairs = phase_rows * length
    groups = send_ref.shape[1]
    full = channels // LANES
    rest = channels - full * LANES
    extra = groups - own_rows * full
    halves = recv_sem.shape[0]
    part_count = count // halves
    part = length // halves
    me = lax.axis_index("row") * cols + lax.axis_index("col")
    my_half = me // part_count
    cut = own_rows // phase_rows // 2 * phase_rows
    staged = halves > 1 and cut > 0
    lead = part_count // 4
    late = my_half > 0 if staged else me < 0

    def place(other):
        return {"row": other // cols, "col": lax.rem(other, cols)}

    def another(step):
        return jnp.where(step < me, step, step + 1)

    def transfer(first, size, source, target, other, half):
        span = pl.ds(first, size)
        return pltpu.make_async_remote_copy(
            src_ref=send_ref.at[source, span],
            dst_ref=land_ref.at[target, span],
            send_sem=send_sem,
            recv_sem=recv_sem.at[half],
            device_id=place(other),
            device_id_type=pl.DeviceIdType.MESH,
        )

    loads = [
        pltpu.make_async_copy(source, target, load_sem.at[index])
        for index, (source, target) in enumerate(
            [
                (w_query_hbm, w_query),
                (w_value_hbm, w_value),
                (w_gate_hbm, w_gate),
                (norm_in_hbm, norm_in),
                (x_hbm, x_ref),
                (w_key_hbm, w_key),
                (w_out_hbm, w_out),
                (norm_mid_hbm, norm_mid),
                (norm_out_hbm, norm_out),
                (w_up_hbm, w_up),
                (w_down_hbm, w_down),
            ]
        )
    ]
    for load in loads[:8]:
        load.start()
    barrier = pltpu.get_barrier_semaphore()

    def signal(semaphore, other):
        pl.semaphore_signal(
            semaphore, inc=1, device_id=place(other), device_id_type=pl.DeviceIdType.MESH
        )

    def send(first, size, other):
        transfer(first, size, other, me, other, my_half).start()

    @pl.loop(0, jnp.where(late, part_count, count - 1))
    def _(step):
        signal(barrier, another(step))

    for load in loads[8:]:
        load.start()
    flip = identity(length)
    for index, weight in enumerate((w_query, w_value, w_gate)):
        loads[index].wait()
        turned_ref[index] = weight[...].T
    for load in loads[3:8]:
        load.wait()
    gain_ref[0] = upright(norm_in[...], phase_pairs)
    gain_ref[1] = upright(norm_mid[...], phase_pairs)
    scale = HEAD_DIM ** (-0.5) * LOG2E
    fold = 2
    reach = LANES // HEAD_DIM
    nothing = jnp.zeros((HEAD_DIM, length), jnp.bfloat16)

    for phase in range(own_rows // phase_rows):
        start = phase * phase_rows
        widened = jnp.concatenate(
            [x_ref[start + inside] for inside in range(phase_rows)], axis=1
        ).astype(jnp.float32)
        normed = normalize(widened, gain_ref[0]).astype(jnp.bfloat16)
        queries = contract(turned_ref[0], normed, 1, 0).astype(jnp.bfloat16)
        values = contract(turned_ref[1], normed, 1, 0).astype(jnp.bfloat16)
        gates = jax.nn.sigmoid(contract(turned_ref[2], normed, 1, 0))
        keys = contract(normed, w_key[...], 0, 0).astype(jnp.bfloat16)
        for inside in range(phase_rows):
            along = slice(inside * length, (inside + 1) * length)
            for head in range(0, HEADS, fold):
                base = head // reach * reach
                spread = jnp.concatenate(
                    [
                        jnp.concatenate(
                            [
                                queries[other * HEAD_DIM : (other + 1) * HEAD_DIM, along]
                                if other == chosen
                                else nothing
                                for other in range(base, base + reach)
                            ],
                            axis=0,
                        )
                        for chosen in range(head, head + fold)
                    ],
                    axis=1,
                )
                group = slice(base * HEAD_DIM, (base + reach) * HEAD_DIM)
                scores = contract(keys[along, group], spread, 1, 0)
                expanded = jnp.exp2((scores - jnp.max(scores, axis=0, keepdims=True)) * scale)
                inverse = 1.0 / jnp.sum(expanded, axis=0, keepdims=True)
                rounded = expanded.astype(jnp.bfloat16)
                for chosen in range(fold):
                    span = slice((head + chosen) * HEAD_DIM, (head + chosen + 1) * HEAD_DIM)
                    over = slice(chosen * length, (chosen + 1) * length)
                    attended = contract(values[span, along], rounded[:, over], 1, 0)
                    merged_ref[span, along] = (
                        attended * inverse[:, over] * gates[span, along]
                    ).astype(jnp.bfloat16)
        update = contract(w_out[...], merged_ref[...], 1, 0)
        rowwise = normalize(widened + update, gain_ref[1]).astype(jnp.bfloat16)
        for inside in range(phase_rows):
            along = slice(inside * length, (inside + 1) * length)
            row_ref[start + inside] = rowwise[:, along]
            if rest:
                rest_ref[start + inside] = rowwise[full * LANES :, along]
            sent = contract(flip, rowwise[: full * LANES, along], 1, 1)
            for group in range(full):
                piece = sent[:, group * LANES : (group + 1) * LANES]
                send_ref[:, (start + inside) * full + group] = piece.reshape(
                    count, own_rows, LANES
                ).astype(jnp.bfloat16)
        row = start + phase_rows - 1

        if staged and row == cut - 1:

            @pl.when(late)
            def _():
                pl.semaphore_wait(barrier, part_count)

                @pl.loop(lead, my_half * part_count)
                def _(other):
                    send(0, cut * full, other)

        if row == own_rows - 1:
            if rest:
                folded = rest_ref[...].reshape(own_rows * rest, length)
                for index in range(extra):
                    held = folded[index * LANES : (index + 1) * LANES]
                    send_ref[:, own_rows * full + index, :, : held.shape[0]] = (
                        contract(flip, held, 1, 1)
                        .reshape(count, own_rows, held.shape[0])
                        .astype(jnp.bfloat16)
                    )

            def send_early():
                pl.semaphore_wait(barrier, count - 1)

                @pl.loop(0, count - 1)
                def _(step):
                    send(0, groups, another(step))

            def send_staged():
                pl.semaphore_wait(barrier, count - 1)
                signal(go_sem, me + part_count)

                @pl.loop(0, part_count)
                def _(step):
                    @pl.when(step < part_count - 1)
                    def _():
                        send(0, groups, another(step))

                    send(0, groups, part_count + step)

            def send_late():
                @pl.loop(0, lead)
                def _(other):
                    send(0, groups, other)

                @pl.loop(lead, my_half * part_count)
                def _(other):
                    send(cut * full, groups - cut * full, other)

                pl.semaphore_wait(go_sem, 1)

                @pl.loop(my_half * part_count, count - 1)
                def _(step):
                    send(0, groups, another(step))

            if staged:
                pl.when(late)(send_late)
                pl.when(jnp.logical_not(late))(send_staged)
            else:
                send_early()

    keep = pltpu.make_async_copy(send_ref.at[me], land_ref.at[me], recv_sem.at[my_half])
    keep.start()
    mirror_ref[...] = mirrored(own_rows, part)
    for half in range(halves):
        own_ref[half] = jnp.concatenate(
            [row_ref[row, :, half * part : (half + 1) * part] for row in range(own_rows)], axis=1
        )
    for load in loads[8:]:
        load.wait()

    @pl.loop(0, w_up.shape[1] // LANES)
    def _(block):
        span = pl.ds(pl.multiple_of(block * LANES, LANES), LANES)
        up_ref[span, :] = w_up[:, span].T

    gain_out = upright(norm_out[...], LANES)[:, :1]
    turn = identity(part)

    @pl.loop(0, halves)
    def _(step):
        half = lax.rem(my_half + step, halves)
        source = pl.ds(half * part_count, part_count)
        transfer(0, groups, source, source, another(0), half).wait_recv()

        def landed(group):
            return land_ref[source, group].astype(jnp.float32).reshape(part, LANES)

        slots = jnp.concatenate(
            [
                jnp.concatenate([landed(row * full + group) for group in range(full)], axis=1)
                for row in range(own_rows)
            ],
            axis=0,
        ).astype(jnp.bfloat16)
        received = contract(slots, mirror_ref[...], 0, 0)
        if rest:
            per = LANES // rest
            pieces = []
            for index in range(extra):
                held = landed(own_rows * full + index).astype(jnp.bfloat16)
                upended = contract(held, turn, 0, 0).astype(jnp.bfloat16)
                for inside in range(min(per, own_rows - index * per)):
                    pieces.append(upended[inside * rest : (inside + 1) * rest])
            tail = contract(jnp.concatenate(pieces, axis=1), mirror_ref[...], 1, 0)
            received = jnp.concatenate([received, tail], axis=0)
        symmetric = ((own_ref[half].astype(jnp.float32) + received) * 0.5).astype(jnp.bfloat16)
        flat = symmetric.astype(jnp.float32)
        inner = normalize(flat, gain_out).astype(jnp.bfloat16)
        hidden = jnp.maximum(contract(up_ref[...], inner, 1, 0), 0.0).astype(jnp.bfloat16)
        own_ref[half] = (flat + contract(w_down[...], hidden, 1, 0)).astype(jnp.bfloat16)

    for row in range(own_rows):
        out_ref[row] = jnp.concatenate(
            [own_ref[half, :, row * part : (row + 1) * part] for half in range(halves)], axis=1
        )
    transfer(0, groups, pl.ds(0, count - 1), pl.ds(0, count - 1), another(0), 0).wait_send()


def local(
    pair_map, norm_in, w_query, w_key, w_value, w_gate, w_out, norm_mid, norm_out, w_up, w_down
):
    cols = lax.axis_size("col")
    count = lax.axis_size("row") * cols
    tile_rows, tile_cols, channels = pair_map.shape
    own_rows = tile_rows // cols
    length = tile_cols * cols
    rows = pair_map
    if cols > 1:
        folds = pair_map.reshape(cols, own_rows, tile_cols, channels)
        rows = lax.all_to_all(folds, "col", split_axis=0, concat_axis=2, tiled=True)[0]
    width = w_query.shape[1]
    phase_rows = 2 if own_rows % 2 == 0 else 1
    halves = 2 if count % 2 == 0 else 1
    part_pairs = own_rows * length // halves
    rest = channels % LANES
    groups = own_rows * (channels // LANES)
    if rest:
        groups += pl.cdiv(own_rows, LANES // rest)
    operands = (
        rows.transpose(0, 2, 1),
        norm_in,
        w_query,
        w_key,
        w_value,
        w_gate,
        w_out.T,
        norm_mid,
        norm_out,
        w_up,
        w_down.T,
    )
    finished = pl.pallas_call(
        functools.partial(block_kernel, count, cols),
        out_shape=pltpu.VMEM((own_rows, channels, length), jnp.bfloat16),
        in_specs=[pl.BlockSpec(memory_space=pl.ANY)] * len(operands),
        out_specs=pl.BlockSpec(memory_space=pltpu.VMEM),
        scratch_shapes=[pltpu.VMEM(operand.shape, operand.dtype) for operand in operands]
        + [
            pltpu.VMEM((3, width, channels), jnp.bfloat16),
            pltpu.VMEM((width, phase_rows * length), jnp.bfloat16),
            pltpu.VMEM((own_rows, channels, length), jnp.bfloat16),
            pltpu.VMEM((halves, channels, part_pairs), jnp.bfloat16),
            pltpu.VMEM((2, channels, phase_rows * length), jnp.float32),
            pltpu.VMEM((own_rows, max(rest, 16), length), jnp.bfloat16),
            pltpu.VMEM((part_pairs, part_pairs), jnp.bfloat16),
            pltpu.VMEM(w_up.shape[::-1], jnp.bfloat16),
            pltpu.VMEM((count, groups, own_rows, LANES), jnp.bfloat16),
            pltpu.VMEM((count, groups, own_rows, LANES), jnp.bfloat16),
            pltpu.SemaphoreType.DMA((len(operands),)),
            pltpu.SemaphoreType.DMA,
            pltpu.SemaphoreType.DMA((halves,)),
            pltpu.SemaphoreType.REGULAR,
        ],
        compiler_params=pltpu.CompilerParams(
            collective_id=0, has_side_effects=True, vmem_limit_bytes=VLIM
        ),
    )(*operands).transpose(0, 2, 1)
    if cols == 1:
        return finished
    returned = lax.all_to_all(
        finished.reshape(own_rows, cols, tile_cols, channels),
        "col",
        split_axis=1,
        concat_axis=0,
        tiled=True,
    )
    return returned.reshape(tile_rows, tile_cols, channels)


VLIM = 62 * MIB


def solution(mesh):
    placed = (P(("grp", "row"), "col", None), P(), P(), P(), P(), P(), P(), P(), P(), P(), P())
    return jax.shard_map(
        local, mesh=mesh, in_specs=placed, out_specs=P(("grp", "row"), "col", None), check_vma=False
    )
```

```python
import functools

import jax
import jax.numpy as jnp
from jax import lax
from jax.experimental import pallas as pl
from jax.experimental.pallas import tpu as pltpu
from jax.sharding import PartitionSpec as P

HEADS = 8
HEAD_DIM = 32
LANES = 128
LOG2E = 1.4426950408889634
MIB = 1 << 20

epsilon = 1e-06


def normalize(inputs, gain):
    mean_square = jnp.mean(inputs * inputs, axis=0, keepdims=True)
    return inputs * lax.rsqrt(mean_square + epsilon) * gain


def contract(left, right, left_dim, right_dim):
    return lax.dot_general(
        left, right, (((left_dim,), (right_dim,)), ((), ())), preferred_element_type=jnp.float32
    )


def upright(gain, pairs):
    column = jnp.broadcast_to(gain[None], (LANES, gain.shape[0])).T
    return jnp.concatenate([column] * (pairs // LANES), axis=1)


def identity(size):
    row = lax.broadcasted_iota(jnp.int32, (size, size), 0)
    column = lax.broadcasted_iota(jnp.int32, (size, size), 1)
    return jnp.where(row == column, 1.0, 0.0).astype(jnp.bfloat16)


def mirrored(own_rows, length):
    shape = (own_rows * length, own_rows * length)
    slot = lax.broadcasted_iota(jnp.int32, shape, 0)
    pair = lax.broadcasted_iota(jnp.int32, shape, 1)
    column = pair % length
    wanted = column % own_rows * length + column // own_rows * own_rows + pair // length
    return jnp.where(slot == wanted, 1.0, 0.0).astype(jnp.bfloat16)


def block_kernel(
    count,
    cols,
    x_hbm,
    norm_in_hbm,
    w_query_hbm,
    w_key_hbm,
    w_value_hbm,
    w_gate_hbm,
    w_out_hbm,
    norm_mid_hbm,
    norm_out_hbm,
    w_up_hbm,
    w_down_hbm,
    parts_ref,
    hidden_ref,
    down_ref,
    x_ref,
    norm_in,
    w_query,
    w_key,
    w_value,
    w_gate,
    w_out,
    norm_mid,
    norm_out,
    w_up,
    turned_ref,
    merged_ref,
    row_ref,
    own_ref,
    gain_ref,
    rest_ref,
    mirror_ref,
    up_ref,
    send_ref,
    land_ref,
    load_sem,
    send_sem,
    recv_sem,
    go_sem,
):
    own_rows, channels, length = x_ref.shape
    phase_rows = 2 if own_rows % 2 == 0 else 1
    phase_pairs = phase_rows * length
    groups = send_ref.shape[1]
    full = channels // LANES
    rest = channels - full * LANES
    extra = groups - own_rows * full
    halves = recv_sem.shape[0]
    part_count = count // halves
    part = length // halves
    me = lax.axis_index("row") * cols + lax.axis_index("col")
    my_half = me // part_count
    cut = own_rows // phase_rows // 2 * phase_rows
    staged = halves > 1 and cut > 0
    lead = part_count // 4
    late = my_half > 0 if staged else me < 0

    def place(other):
        if cols == 1:
            return {"row": other}
        return {"row": other // cols, "col": lax.rem(other, cols)}

    def another(step):
        return jnp.where(step < me, step, step + 1)

    def transfer(first, size, source, target, other, half):
        span = pl.ds(first, size)
        return pltpu.make_async_remote_copy(
            src_ref=send_ref.at[source, span],
            dst_ref=land_ref.at[target, span],
            send_sem=send_sem,
            recv_sem=recv_sem.at[half],
            device_id=place(other),
            device_id_type=pl.DeviceIdType.MESH,
        )

    loads = [
        pltpu.make_async_copy(source, target, load_sem.at[index])
        for index, (source, target) in enumerate(
            [
                (w_query_hbm, w_query),
                (w_value_hbm, w_value),
                (w_gate_hbm, w_gate),
                (norm_in_hbm, norm_in),
                (x_hbm, x_ref),
                (w_key_hbm, w_key),
                (w_out_hbm, w_out),
                (norm_mid_hbm, norm_mid),
                (norm_out_hbm, norm_out),
                (w_up_hbm, w_up),
                (w_down_hbm, down_ref),
            ]
        )
    ]
    for load in loads[:8]:
        load.start()
    barrier = pltpu.get_barrier_semaphore()

    def signal(semaphore, other):
        pl.semaphore_signal(
            semaphore, inc=1, device_id=place(other), device_id_type=pl.DeviceIdType.MESH
        )

    def send(first, size, other):
        transfer(first, size, other, me, other, my_half).start()

    @pl.loop(0, jnp.where(late, part_count, count - 1))
    def _(step):
        signal(barrier, another(step))

    for load in loads[8:]:
        load.start()
    flip = identity(length)
    for index, weight in enumerate((w_query, w_value, w_gate)):
        loads[index].wait()
        turned_ref[index] = weight[...].T
    for load in loads[3:8]:
        load.wait()
    gain_ref[0] = upright(norm_in[...], phase_pairs)
    gain_ref[1] = upright(norm_mid[...], phase_pairs)
    scale = HEAD_DIM ** (-0.5) * LOG2E
    fold = 2
    reach = LANES // HEAD_DIM
    nothing = jnp.zeros((HEAD_DIM, length), jnp.bfloat16)

    for phase in range(own_rows // phase_rows):
        start = phase * phase_rows
        widened = jnp.concatenate(
            [x_ref[start + inside] for inside in range(phase_rows)], axis=1
        ).astype(jnp.float32)
        normed = normalize(widened, gain_ref[0]).astype(jnp.bfloat16)
        queries = contract(turned_ref[0], normed, 1, 0).astype(jnp.bfloat16)
        values = contract(turned_ref[1], normed, 1, 0).astype(jnp.bfloat16)
        gates = jax.nn.sigmoid(contract(turned_ref[2], normed, 1, 0))
        keys = contract(normed, w_key[...], 0, 0).astype(jnp.bfloat16)
        for inside in range(phase_rows):
            along = slice(inside * length, (inside + 1) * length)
            for head in range(0, HEADS, fold):
                base = head // reach * reach
                spread = jnp.concatenate(
                    [
                        jnp.concatenate(
                            [
                                queries[other * HEAD_DIM : (other + 1) * HEAD_DIM, along]
                                if other == chosen
                                else nothing
                                for other in range(base, base + reach)
                            ],
                            axis=0,
                        )
                        for chosen in range(head, head + fold)
                    ],
                    axis=1,
                )
                group = slice(base * HEAD_DIM, (base + reach) * HEAD_DIM)
                scores = contract(keys[along, group], spread, 1, 0)
                expanded = jnp.exp2((scores - jnp.max(scores, axis=0, keepdims=True)) * scale)
                inverse = 1.0 / jnp.sum(expanded, axis=0, keepdims=True)
                rounded = expanded.astype(jnp.bfloat16)
                for chosen in range(fold):
                    span = slice((head + chosen) * HEAD_DIM, (head + chosen + 1) * HEAD_DIM)
                    over = slice(chosen * length, (chosen + 1) * length)
                    attended = contract(values[span, along], rounded[:, over], 1, 0)
                    merged_ref[span, along] = (
                        attended * inverse[:, over] * gates[span, along]
                    ).astype(jnp.bfloat16)
        update = contract(w_out[...], merged_ref[...], 1, 0)
        rowwise = normalize(widened + update, gain_ref[1]).astype(jnp.bfloat16)
        for inside in range(phase_rows):
            along = slice(inside * length, (inside + 1) * length)
            row_ref[start + inside] = rowwise[:, along]
            if rest:
                rest_ref[start + inside] = rowwise[full * LANES :, along]
            sent = contract(flip, rowwise[: full * LANES, along], 1, 1)
            for group in range(full):
                piece = sent[:, group * LANES : (group + 1) * LANES]
                send_ref[:, (start + inside) * full + group] = piece.reshape(
                    count, own_rows, LANES
                ).astype(jnp.bfloat16)
        row = start + phase_rows - 1

        if staged and row == cut - 1:

            @pl.when(late)
            def _():
                pl.semaphore_wait(barrier, part_count)

                @pl.loop(lead, my_half * part_count)
                def _(other):
                    send(0, cut * full, other)

        if row == own_rows - 1:
            if rest:
                folded = rest_ref[...].reshape(own_rows * rest, length)
                for index in range(extra):
                    held = folded[index * LANES : (index + 1) * LANES]
                    send_ref[:, own_rows * full + index, :, : held.shape[0]] = (
                        contract(flip, held, 1, 1)
                        .reshape(count, own_rows, held.shape[0])
                        .astype(jnp.bfloat16)
                    )

            def send_early():
                pl.semaphore_wait(barrier, count - 1)

                @pl.loop(0, count - 1)
                def _(step):
                    send(0, groups, another(step))

            def send_staged():
                pl.semaphore_wait(barrier, count - 1)
                signal(go_sem, me + part_count)

                @pl.loop(0, part_count)
                def _(step):
                    @pl.when(step < part_count - 1)
                    def _():
                        send(0, groups, another(step))

                    send(0, groups, part_count + step)

            def send_late():
                @pl.loop(0, lead)
                def _(other):
                    send(0, groups, other)

                @pl.loop(lead, my_half * part_count)
                def _(other):
                    send(cut * full, groups - cut * full, other)

                pl.semaphore_wait(go_sem, 1)

                @pl.loop(my_half * part_count, count - 1)
                def _(step):
                    send(0, groups, another(step))

            if staged:
                pl.when(late)(send_late)
                pl.when(jnp.logical_not(late))(send_staged)
            else:
                send_early()

    keep = pltpu.make_async_copy(send_ref.at[me], land_ref.at[me], recv_sem.at[my_half])
    keep.start()
    mirror_ref[...] = mirrored(own_rows, part)
    for half in range(halves):
        own_ref[half] = jnp.concatenate(
            [row_ref[row, :, half * part : (half + 1) * part] for row in range(own_rows)], axis=1
        )
    for load in loads[8:]:
        load.wait()

    @pl.loop(0, w_up.shape[1] // LANES)
    def _(block):
        span = pl.ds(pl.multiple_of(block * LANES, LANES), LANES)
        up_ref[span, :] = w_up[:, span].T

    gain_out = upright(norm_out[...], LANES)[:, :1]
    turn = identity(part)

    @pl.loop(0, halves)
    def _(step):
        half = lax.rem(my_half + step, halves)
        source = pl.ds(half * part_count, part_count)
        transfer(0, groups, source, source, another(0), half).wait_recv()

        def landed(group):
            return land_ref[source, group].astype(jnp.float32).reshape(part, LANES)

        slots = jnp.concatenate(
            [
                jnp.concatenate([landed(row * full + group) for group in range(full)], axis=1)
                for row in range(own_rows)
            ],
            axis=0,
        ).astype(jnp.bfloat16)
        received = contract(slots, mirror_ref[...], 0, 0)
        if rest:
            per = LANES // rest
            pieces = []
            for index in range(extra):
                held = landed(own_rows * full + index).astype(jnp.bfloat16)
                upended = contract(held, turn, 0, 0).astype(jnp.bfloat16)
                for inside in range(min(per, own_rows - index * per)):
                    pieces.append(upended[inside * rest : (inside + 1) * rest])
            tail = contract(jnp.concatenate(pieces, axis=1), mirror_ref[...], 1, 0)
            received = jnp.concatenate([received, tail], axis=0)
        symmetric = ((own_ref[half].astype(jnp.float32) + received) * 0.5).astype(jnp.bfloat16)
        flat = symmetric.astype(jnp.float32)
        inner = normalize(flat, gain_out).astype(jnp.bfloat16)
        hidden_ref[...] = jnp.maximum(contract(up_ref[...], inner, 1, 0), 0.0).astype(jnp.bfloat16)
        parts_ref[half] = symmetric

        @pl.when(step < halves - 1)
        def _():
            parts_ref[half] = (flat + contract(down_ref[...], hidden_ref[...], 1, 0)).astype(
                jnp.bfloat16
            )

    transfer(0, groups, pl.ds(0, count - 1), pl.ds(0, count - 1), another(0), 0).wait_send()


def finish_kernel(count, cols, parts_ref, hidden_ref, down_ref, out_ref, row_ref, sem):
    own_rows, channels, length = row_ref.shape
    halves = parts_ref.shape[0]
    part = length // halves
    me = lax.axis_index("row") * cols + lax.axis_index("col")
    half = lax.rem(me // (count // halves) + halves - 1, halves)
    result = (
        parts_ref[half].astype(jnp.float32) + contract(down_ref[...], hidden_ref[...], 1, 0)
    ).astype(jnp.bfloat16)
    held = [jnp.where(half == other, result, parts_ref[other]) for other in range(halves)]
    copies = []
    for row in range(own_rows):
        row_ref[row] = jnp.concatenate(
            [block[:, row * part : (row + 1) * part] for block in held], axis=1
        )
        copies.append(pltpu.make_async_copy(row_ref.at[row], out_ref.at[row], sem.at[row]))
        copies[-1].start()
    for copy in copies:
        copy.wait()


def local(
    pair_map, norm_in, w_query, w_key, w_value, w_gate, w_out, norm_mid, norm_out, w_up, w_down
):
    cols = lax.axis_size("col")
    count = lax.axis_size("row") * cols
    tile_rows, tile_cols, channels = pair_map.shape
    own_rows = tile_rows // cols
    length = tile_cols * cols
    rows = pair_map
    if cols > 1:
        folds = pair_map.reshape(cols, own_rows, tile_cols, channels)
        rows = lax.all_to_all(folds, "col", split_axis=0, concat_axis=2, tiled=True)[0]
    width = w_query.shape[1]
    phase_rows = 2 if own_rows % 2 == 0 else 1
    halves = 2 if count % 2 == 0 else 1
    part_pairs = own_rows * length // halves
    rest = channels % LANES
    groups = own_rows * (channels // LANES)
    if rest:
        groups += pl.cdiv(own_rows, LANES // rest)
    operands = (
        rows.transpose(0, 2, 1),
        norm_in,
        w_query,
        w_key,
        w_value,
        w_gate,
        w_out.T,
        norm_mid,
        norm_out,
        w_up,
        w_down.T,
    )
    parts, hidden, down = pl.pallas_call(
        functools.partial(block_kernel, count, cols),
        out_shape=(
            pltpu.VMEM((halves, channels, part_pairs), jnp.bfloat16),
            pltpu.VMEM((w_up.shape[1], part_pairs), jnp.bfloat16),
            pltpu.VMEM(w_down.shape[::-1], jnp.bfloat16),
        ),
        in_specs=[pl.BlockSpec(memory_space=pl.ANY)] * len(operands),
        out_specs=[pl.BlockSpec(memory_space=pltpu.VMEM)] * 3,
        scratch_shapes=[pltpu.VMEM(operand.shape, operand.dtype) for operand in operands[:-1]]
        + [
            pltpu.VMEM((3, width, channels), jnp.bfloat16),
            pltpu.VMEM((width, phase_rows * length), jnp.bfloat16),
            pltpu.VMEM((own_rows, channels, length), jnp.bfloat16),
            pltpu.VMEM((halves, channels, part_pairs), jnp.bfloat16),
            pltpu.VMEM((2, channels, phase_rows * length), jnp.float32),
            pltpu.VMEM((own_rows, max(rest, 16), length), jnp.bfloat16),
            pltpu.VMEM((part_pairs, part_pairs), jnp.bfloat16),
            pltpu.VMEM(w_up.shape[::-1], jnp.bfloat16),
            pltpu.VMEM((count, groups, own_rows, LANES), jnp.bfloat16),
            pltpu.VMEM((count, groups, own_rows, LANES), jnp.bfloat16),
            pltpu.SemaphoreType.DMA((len(operands),)),
            pltpu.SemaphoreType.DMA,
            pltpu.SemaphoreType.DMA((halves,)),
            pltpu.SemaphoreType.REGULAR,
        ],
        compiler_params=pltpu.CompilerParams(
            collective_id=0, has_side_effects=True, vmem_limit_bytes=VLIM
        ),
    )(*operands)
    finished = pl.pallas_call(
        functools.partial(finish_kernel, count, cols),
        out_shape=jax.ShapeDtypeStruct((own_rows, channels, length), jnp.bfloat16),
        in_specs=[pl.BlockSpec(memory_space=pltpu.VMEM)] * 3,
        out_specs=pl.BlockSpec(memory_space=pl.ANY),
        scratch_shapes=[
            pltpu.VMEM((own_rows, channels, length), jnp.bfloat16),
            pltpu.SemaphoreType.DMA((own_rows,)),
        ],
        compiler_params=pltpu.CompilerParams(vmem_limit_bytes=16 * MIB),
    )(parts, hidden, down).transpose(0, 2, 1)
    if cols == 1:
        return finished
    returned = lax.all_to_all(
        finished.reshape(own_rows, cols, tile_cols, channels),
        "col",
        split_axis=1,
        concat_axis=0,
        tiled=True,
    )
    return returned.reshape(tile_rows, tile_cols, channels)


VLIM = 61 * MIB


def solution(mesh):
    placed = (P(("grp", "row"), "col", None), P(), P(), P(), P(), P(), P(), P(), P(), P(), P())
    return jax.shard_map(
        local, mesh=mesh, in_specs=placed, out_specs=P(("grp", "row"), "col", None), check_vma=False
    )
```

```python
import functools

import jax
import jax.numpy as jnp
from jax import lax
from jax.experimental import pallas as pl
from jax.experimental.pallas import tpu as pltpu
from jax.sharding import PartitionSpec as P

HEADS = 8
HEAD_DIM = 32
LANES = 128
LOG2E = 1.4426950408889634
MIB = 1 << 20

epsilon = 1e-06


def normalize(inputs, gain):
    mean_square = jnp.mean(inputs * inputs, axis=0, keepdims=True)
    return inputs * lax.rsqrt(mean_square + epsilon) * gain


def contract(left, right, left_dim, right_dim):
    return lax.dot_general(
        left, right, (((left_dim,), (right_dim,)), ((), ())), preferred_element_type=jnp.float32
    )


def upright(gain, pairs):
    column = jnp.broadcast_to(gain[None], (LANES, gain.shape[0])).T
    return jnp.concatenate([column] * (pairs // LANES), axis=1)


def identity(size):
    row = lax.broadcasted_iota(jnp.int32, (size, size), 0)
    column = lax.broadcasted_iota(jnp.int32, (size, size), 1)
    return jnp.where(row == column, 1.0, 0.0).astype(jnp.bfloat16)


def mirrored(own_rows, length):
    shape = (own_rows * length, own_rows * length)
    slot = lax.broadcasted_iota(jnp.int32, shape, 0)
    pair = lax.broadcasted_iota(jnp.int32, shape, 1)
    column = pair % length
    wanted = column % own_rows * length + column // own_rows * own_rows + pair // length
    return jnp.where(slot == wanted, 1.0, 0.0).astype(jnp.bfloat16)


def block_kernel(
    count,
    cols,
    x_hbm,
    norm_in_hbm,
    w_query_hbm,
    w_key_hbm,
    w_value_hbm,
    w_gate_hbm,
    w_out_hbm,
    norm_mid_hbm,
    norm_out_hbm,
    w_up_hbm,
    w_down_hbm,
    parts_ref,
    hidden_ref,
    down_ref,
    x_ref,
    norm_in,
    w_query,
    w_key,
    w_value,
    w_gate,
    w_out,
    norm_mid,
    norm_out,
    w_up,
    turned_ref,
    merged_ref,
    row_ref,
    own_ref,
    gain_ref,
    rest_ref,
    mirror_ref,
    up_ref,
    send_ref,
    land_ref,
    load_sem,
    send_sem,
    recv_sem,
    go_sem,
):
    own_rows, channels, length = x_ref.shape
    phase_rows = 2 if own_rows % 2 == 0 else 1
    phase_pairs = phase_rows * length
    groups = send_ref.shape[1]
    full = channels // LANES
    rest = channels - full * LANES
    extra = groups - own_rows * full
    halves = recv_sem.shape[0]
    part_count = count // halves
    part = length // halves
    me = lax.axis_index("row") * cols + lax.axis_index("col")
    my_half = me // part_count
    cut = own_rows // phase_rows // 2 * phase_rows
    staged = halves > 1 and cut > 0
    lead = part_count // 4
    late = my_half > 0 if staged else me < 0

    def place(other):
        if cols == 1:
            return {"row": other}
        return {"row": other // cols, "col": lax.rem(other, cols)}

    def another(step):
        return jnp.where(step < me, step, step + 1)

    def transfer(first, size, source, target, other, half):
        span = pl.ds(first, size)
        return pltpu.make_async_remote_copy(
            src_ref=send_ref.at[source, span],
            dst_ref=land_ref.at[target, span],
            send_sem=send_sem,
            recv_sem=recv_sem.at[half],
            device_id=place(other),
            device_id_type=pl.DeviceIdType.MESH,
        )

    loads = [
        pltpu.make_async_copy(source, target, load_sem.at[index])
        for index, (source, target) in enumerate(
            [
                (w_query_hbm, w_query),
                (w_value_hbm, w_value),
                (w_gate_hbm, w_gate),
                (norm_in_hbm, norm_in),
                (x_hbm, x_ref),
                (w_key_hbm, w_key),
                (w_out_hbm, w_out),
                (norm_mid_hbm, norm_mid),
                (norm_out_hbm, norm_out),
                (w_up_hbm, w_up),
                (w_down_hbm, down_ref),
            ]
        )
    ]
    for load in loads[:8]:
        load.start()
    barrier = pltpu.get_barrier_semaphore()

    def signal(semaphore, other):
        pl.semaphore_signal(
            semaphore, inc=1, device_id=place(other), device_id_type=pl.DeviceIdType.MESH
        )

    def send(first, size, other):
        transfer(first, size, other, me, other, my_half).start()

    @pl.loop(0, jnp.where(late, part_count, count - 1))
    def _(step):
        signal(barrier, another(step))

    for load in loads[8:]:
        load.start()
    flip = identity(length)
    for index, weight in enumerate((w_query, w_value, w_gate)):
        loads[index].wait()
        turned_ref[index] = weight[...].T
    for load in loads[3:8]:
        load.wait()
    gain_ref[0] = upright(norm_in[...], phase_pairs)
    gain_ref[1] = upright(norm_mid[...], phase_pairs)
    scale = HEAD_DIM ** (-0.5) * LOG2E
    fold = 2
    reach = LANES // HEAD_DIM
    nothing = jnp.zeros((HEAD_DIM, length), jnp.bfloat16)

    for phase in range(own_rows // phase_rows):
        start = phase * phase_rows
        widened = jnp.concatenate(
            [x_ref[start + inside] for inside in range(phase_rows)], axis=1
        ).astype(jnp.float32)
        normed = normalize(widened, gain_ref[0]).astype(jnp.bfloat16)
        queries = contract(turned_ref[0], normed, 1, 0).astype(jnp.bfloat16)
        values = contract(turned_ref[1], normed, 1, 0).astype(jnp.bfloat16)
        gates = jax.nn.sigmoid(contract(turned_ref[2], normed, 1, 0))
        keys = contract(normed, w_key[...], 0, 0).astype(jnp.bfloat16)
        for inside in range(phase_rows):
            along = slice(inside * length, (inside + 1) * length)
            for head in range(0, HEADS, fold):
                base = head // reach * reach
                spread = jnp.concatenate(
                    [
                        jnp.concatenate(
                            [
                                queries[other * HEAD_DIM : (other + 1) * HEAD_DIM, along]
                                if other == chosen
                                else nothing
                                for other in range(base, base + reach)
                            ],
                            axis=0,
                        )
                        for chosen in range(head, head + fold)
                    ],
                    axis=1,
                )
                group = slice(base * HEAD_DIM, (base + reach) * HEAD_DIM)
                scores = contract(keys[along, group], spread, 1, 0)
                expanded = jnp.exp2(scores * scale - jnp.max(scores, axis=0, keepdims=True) * scale)
                inverse = 1.0 / jnp.sum(expanded, axis=0, keepdims=True)
                rounded = expanded.astype(jnp.bfloat16)
                for chosen in range(fold):
                    span = slice((head + chosen) * HEAD_DIM, (head + chosen + 1) * HEAD_DIM)
                    over = slice(chosen * length, (chosen + 1) * length)
                    attended = contract(values[span, along], rounded[:, over], 1, 0)
                    merged_ref[span, along] = (
                        attended * inverse[:, over] * gates[span, along]
                    ).astype(jnp.bfloat16)
        update = contract(w_out[...], merged_ref[...], 1, 0)
        rowwise = normalize(widened + update, gain_ref[1]).astype(jnp.bfloat16)
        for inside in range(phase_rows):
            along = slice(inside * length, (inside + 1) * length)
            row_ref[start + inside] = rowwise[:, along]
            if rest:
                rest_ref[start + inside] = rowwise[full * LANES :, along]
            sent = contract(flip, rowwise[: full * LANES, along], 1, 1)
            for group in range(full):
                piece = sent[:, group * LANES : (group + 1) * LANES]
                send_ref[:, (start + inside) * full + group] = piece.reshape(
                    count, own_rows, LANES
                ).astype(jnp.bfloat16)
        row = start + phase_rows - 1

        if staged and row == cut - 1:

            @pl.when(late)
            def _():
                pl.semaphore_wait(barrier, part_count)

                @pl.loop(lead, my_half * part_count)
                def _(other):
                    send(0, cut * full, other)

        if row == own_rows - 1:
            if rest:
                folded = rest_ref[...].reshape(own_rows * rest, length)
                for index in range(extra):
                    held = folded[index * LANES : (index + 1) * LANES]
                    send_ref[:, own_rows * full + index, :, : held.shape[0]] = (
                        contract(flip, held, 1, 1)
                        .reshape(count, own_rows, held.shape[0])
                        .astype(jnp.bfloat16)
                    )

            def send_early():
                pl.semaphore_wait(barrier, count - 1)

                @pl.loop(0, count - 1)
                def _(step):
                    send(0, groups, another(step))

            def send_staged():
                pl.semaphore_wait(barrier, count - 1)
                signal(go_sem, me + part_count)

                @pl.loop(0, part_count)
                def _(step):
                    @pl.when(step < part_count - 1)
                    def _():
                        send(0, groups, another(step))

                    send(0, groups, part_count + step)

            def send_late():
                @pl.loop(0, lead)
                def _(other):
                    send(0, groups, other)

                @pl.loop(lead, my_half * part_count)
                def _(other):
                    send(cut * full, groups - cut * full, other)

                pl.semaphore_wait(go_sem, 1)

                @pl.loop(my_half * part_count, count - 1)
                def _(step):
                    send(0, groups, another(step))

            if staged:
                pl.when(late)(send_late)
                pl.when(jnp.logical_not(late))(send_staged)
            else:
                send_early()

    keep = pltpu.make_async_copy(send_ref.at[me], land_ref.at[me], recv_sem.at[my_half])
    keep.start()
    mirror_ref[...] = mirrored(own_rows, part)
    for half in range(halves):
        own_ref[half] = jnp.concatenate(
            [row_ref[row, :, half * part : (half + 1) * part] for row in range(own_rows)], axis=1
        )
    for load in loads[8:]:
        load.wait()

    @pl.loop(0, w_up.shape[1] // LANES)
    def _(block):
        span = pl.ds(pl.multiple_of(block * LANES, LANES), LANES)
        up_ref[span, :] = w_up[:, span].T

    gain_out = upright(norm_out[...], LANES)[:, :1]
    turn = identity(part)

    @pl.loop(0, halves)
    def _(step):
        half = lax.rem(my_half + step, halves)
        source = pl.ds(half * part_count, part_count)
        transfer(0, groups, source, source, another(0), half).wait_recv()

        def landed(group):
            return land_ref[source, group].astype(jnp.float32).reshape(part, LANES)

        slots = jnp.concatenate(
            [
                jnp.concatenate([landed(row * full + group) for group in range(full)], axis=1)
                for row in range(own_rows)
            ],
            axis=0,
        ).astype(jnp.bfloat16)
        received = contract(slots, mirror_ref[...], 0, 0)
        if rest:
            per = LANES // rest
            pieces = []
            for index in range(extra):
                held = landed(own_rows * full + index).astype(jnp.bfloat16)
                upended = contract(held, turn, 0, 0).astype(jnp.bfloat16)
                for inside in range(min(per, own_rows - index * per)):
                    pieces.append(upended[inside * rest : (inside + 1) * rest])
            tail = contract(jnp.concatenate(pieces, axis=1), mirror_ref[...], 1, 0)
            received = jnp.concatenate([received, tail], axis=0)
        symmetric = ((own_ref[half].astype(jnp.float32) + received) * 0.5).astype(jnp.bfloat16)
        flat = symmetric.astype(jnp.float32)
        inner = normalize(flat, gain_out).astype(jnp.bfloat16)
        hidden_ref[...] = jnp.maximum(contract(up_ref[...], inner, 1, 0), 0.0).astype(jnp.bfloat16)
        parts_ref[half] = symmetric

        @pl.when(step < halves - 1)
        def _():
            parts_ref[half] = (flat + contract(down_ref[...], hidden_ref[...], 1, 0)).astype(
                jnp.bfloat16
            )

    transfer(0, groups, pl.ds(0, count - 1), pl.ds(0, count - 1), another(0), 0).wait_send()


def finish_kernel(count, cols, parts_ref, hidden_ref, down_ref, out_ref, row_ref, sem):
    own_rows, channels, length = row_ref.shape
    halves = parts_ref.shape[0]
    part = length // halves
    me = lax.axis_index("row") * cols + lax.axis_index("col")
    half = lax.rem(me // (count // halves) + halves - 1, halves)
    result = (
        parts_ref[half].astype(jnp.float32) + contract(down_ref[...], hidden_ref[...], 1, 0)
    ).astype(jnp.bfloat16)
    held = [jnp.where(half == other, result, parts_ref[other]) for other in range(halves)]
    copies = []
    for row in range(own_rows):
        row_ref[row] = jnp.concatenate(
            [block[:, row * part : (row + 1) * part] for block in held], axis=1
        )
        copies.append(pltpu.make_async_copy(row_ref.at[row], out_ref.at[row], sem.at[row]))
        copies[-1].start()
    for copy in copies:
        copy.wait()


def local(
    pair_map, norm_in, w_query, w_key, w_value, w_gate, w_out, norm_mid, norm_out, w_up, w_down
):
    cols = lax.axis_size("col")
    count = lax.axis_size("row") * cols
    tile_rows, tile_cols, channels = pair_map.shape
    own_rows = tile_rows // cols
    length = tile_cols * cols
    rows = pair_map
    if cols > 1:
        folds = pair_map.reshape(cols, own_rows, tile_cols, channels)
        rows = lax.all_to_all(folds, "col", split_axis=0, concat_axis=2, tiled=True)[0]
    width = w_query.shape[1]
    phase_rows = 2 if own_rows % 2 == 0 else 1
    halves = 2 if count % 2 == 0 else 1
    part_pairs = own_rows * length // halves
    rest = channels % LANES
    groups = own_rows * (channels // LANES)
    if rest:
        groups += pl.cdiv(own_rows, LANES // rest)
    operands = (
        rows.transpose(0, 2, 1),
        norm_in,
        w_query,
        w_key,
        w_value,
        w_gate,
        w_out.T,
        norm_mid,
        norm_out,
        w_up,
        w_down.T,
    )
    parts, hidden, down = pl.pallas_call(
        functools.partial(block_kernel, count, cols),
        out_shape=(
            pltpu.VMEM((halves, channels, part_pairs), jnp.bfloat16),
            pltpu.VMEM((w_up.shape[1], part_pairs), jnp.bfloat16),
            pltpu.VMEM(w_down.shape[::-1], jnp.bfloat16),
        ),
        in_specs=[pl.BlockSpec(memory_space=pl.ANY)] * len(operands),
        out_specs=[pl.BlockSpec(memory_space=pltpu.VMEM)] * 3,
        scratch_shapes=[pltpu.VMEM(operand.shape, operand.dtype) for operand in operands[:-1]]
        + [
            pltpu.VMEM((3, width, channels), jnp.bfloat16),
            pltpu.VMEM((width, phase_rows * length), jnp.bfloat16),
            pltpu.VMEM((own_rows, channels, length), jnp.bfloat16),
            pltpu.VMEM((halves, channels, part_pairs), jnp.bfloat16),
            pltpu.VMEM((2, channels, phase_rows * length), jnp.float32),
            pltpu.VMEM((own_rows, max(rest, 16), length), jnp.bfloat16),
            pltpu.VMEM((part_pairs, part_pairs), jnp.bfloat16),
            pltpu.VMEM(w_up.shape[::-1], jnp.bfloat16),
            pltpu.VMEM((count, groups, own_rows, LANES), jnp.bfloat16),
            pltpu.VMEM((count, groups, own_rows, LANES), jnp.bfloat16),
            pltpu.SemaphoreType.DMA((len(operands),)),
            pltpu.SemaphoreType.DMA,
            pltpu.SemaphoreType.DMA((halves,)),
            pltpu.SemaphoreType.REGULAR,
        ],
        compiler_params=pltpu.CompilerParams(
            collective_id=0, has_side_effects=True, vmem_limit_bytes=VLIM
        ),
    )(*operands)
    finished = pl.pallas_call(
        functools.partial(finish_kernel, count, cols),
        out_shape=jax.ShapeDtypeStruct((own_rows, channels, length), jnp.bfloat16),
        in_specs=[pl.BlockSpec(memory_space=pltpu.VMEM)] * 3,
        out_specs=pl.BlockSpec(memory_space=pl.ANY),
        scratch_shapes=[
            pltpu.VMEM((own_rows, channels, length), jnp.bfloat16),
            pltpu.SemaphoreType.DMA((own_rows,)),
        ],
        compiler_params=pltpu.CompilerParams(vmem_limit_bytes=16 * MIB),
    )(parts, hidden, down).transpose(0, 2, 1)
    if cols == 1:
        return finished
    returned = lax.all_to_all(
        finished.reshape(own_rows, cols, tile_cols, channels),
        "col",
        split_axis=1,
        concat_axis=0,
        tiled=True,
    )
    return returned.reshape(tile_rows, tile_cols, channels)


VLIM = 61 * MIB


def solution(mesh):
    placed = (P(("grp", "row"), "col", None), P(), P(), P(), P(), P(), P(), P(), P(), P(), P())
    return jax.shard_map(
        local, mesh=mesh, in_specs=placed, out_specs=P(("grp", "row"), "col", None), check_vma=False
    )
```
